32 devices in a mesh: pipe: 2 (over x), dp: 4 (over z), tensor: 4 (over y, core).
Axes of the slice: x: 2, y: 2, z: 4, core: 2. Of those that a mesh axis runs over, the one named last changes fastest.
Arguments:
- act_in: bfloat16 [2, 512, 4096], P('pipe', ('dp', 'tensor')), may hold values from -6 to 6
- act_first: bfloat16 [512, 4096], P(('dp', 'tensor')), may hold values from -6 to 6
- grad_in: bfloat16 [2, 512, 4096], P('pipe', ('dp', 'tensor')), may hold values from -1.5 to 1.5
- grad_last: bfloat16 [512, 4096], P(('dp', 'tensor')), may hold values from -1.5 to 1.5
- stash_local: bfloat16 [2, 2, 512, 4096], P('pipe', None, ('dp', 'tensor')), may hold values from -6 to 6
- stash_guest: bfloat16 [2, 2, 3, 512, 512], P('pipe', None, None, ('dp', 'tensor')), may hold values from -6 to 6
- plan: int32 [2, 2, 1, 4], replicated, may hold values from 0 to 7, as said below
- norm_gain: float32 [2, 4096], P('pipe'), may hold values from 0.25 to 1.75
- w_up: bfloat16 [2, 4096, 11264], P('pipe', 'dp', 'tensor'), may hold values from -0.09375 to 0.09375
- w_down: bfloat16 [2, 11264, 4096], P('pipe', 'tensor', 'dp'), may hold values from -0.0546875 to 0.0546875
Outputs:
- act_out: bfloat16 [2, 2, 512, 4096], P('pipe', None, ('dp', 'tensor'))
- grad_out: bfloat16 [2, 2, 512, 4096], P('pipe', None, ('dp', 'tensor'))
- keep_out: bfloat16 [2, 2, 512, 4096], P('pipe', None, ('dp', 'tensor'))
- guest_out: bfloat16 [2, 2, 3, 512, 512], P('pipe', None, None, ('dp', 'tensor'))
- grad_up: bfloat16 [2, 4096, 11264], P('pipe', 'dp', 'tensor')
- grad_down: bfloat16 [2, 11264, 4096], P('pipe', 'tensor', 'dp')
- grad_gain: float32 [2, 4096], P('pipe')
The draws below stay inside these ranges and needn't reach their ends.
Inputs may be any that keep to these rules, and one draw needn't show every extreme that they name: For each first index o and tick m, plan[o, m, s, 0] over s = 0 .. 0 is a permutation of 0 .. 0, with plan[o, 0, 0, 0] = 0, and plan[o, m, s, 1 ..] are 3 distinct block ids below 8.
All inputs are finite; a program needn't handle non-finite values.
Results may differ from the reference program's by a relative error of at most 0.02.
Values may be sent and summed in bfloat16 or wider, within the bound.
A program may use at most 192 MiB of HBM per device.

```python
import jax
import jax.numpy as jnp
from jax import lax

D = 4096
FF = 11264
BW = 512
EVICT = 3
MICRO = 2
SECTIONS = 2
HALF = 1
ROWS = 512
BLOCKS = 8


def draw_plan(key, part):
    first_key = jax.random.fold_in(key, 11)
    second_key = jax.random.fold_in(key, 23)
    partner_scores = jax.random.randint(first_key, (2, MICRO, HALF), 0, 1 << 20) * HALF + jnp.arange(HALF, dtype=jnp.int32)
    partners = jnp.argsort(partner_scores, axis=-1, stable=True).astype(jnp.int32)
    first_tick = partners[:, 0, :]
    last_value = first_tick[:, HALF - 1]
    swapped = jnp.where(first_tick == 0, last_value[:, None], first_tick)
    swapped = swapped.at[:, HALF - 1].set(0)
    partners = partners.at[:, 0, :].set(swapped)
    block_scores = jax.random.randint(second_key, (2, MICRO, HALF, BLOCKS), 0, 1 << 20) * BLOCKS + jnp.arange(BLOCKS, dtype=jnp.int32)
    chosen = jnp.argsort(block_scores, axis=-1, stable=True)[..., :EVICT].astype(jnp.int32)
    return jnp.concatenate([partners[..., None], chosen], axis=-1)


def block_scale(stream_key, extent, shards, smallest, largest):
    loudness, own = 1.0, jax.random.fold_in(stream_key, 6)
    for axis_at, parts in shards:
        draws = jnp.exp(jax.random.uniform(jax.random.fold_in(own, axis_at), (parts,), jnp.float32, smallest / len(shards), largest / len(shards)))
        loudness = loudness * jnp.repeat(draws, extent[axis_at] // parts).reshape([-1 if axis == axis_at else 1 for axis in range(len(extent))])
    return loudness


def centred(key, dims, deviation, most, split=(), kind=jnp.bfloat16):
    values = jax.random.normal(key, dims, jnp.float32) * deviation
    if len(split) > 0:
        values = block_scale(key, dims, split, -0.22, 0.18) * values
    return jnp.clip(values, min=-most, max=most).astype(kind)


def setup_inputs(seed: int = 0) -> dict:
    splits = jax.random.split(jax.random.key(seed), 11)
    act_in = centred(splits[0], (SECTIONS, ROWS, D), 1.0, 6.0, ((0, 2), (1, 16)))
    act_first = centred(splits[1], (ROWS, D), 1.0, 6.0, ((0, 16),))
    grad_in = centred(splits[2], (SECTIONS, ROWS, D), 0.25, 1.5, ((0, 2), (1, 16)))
    grad_last = centred(splits[3], (ROWS, D), 0.25, 1.5, ((0, 16),))
    stash_local = centred(splits[4], (SECTIONS, MICRO, ROWS, D), 1.0, 6.0, ((0, 2), (2, 16)))
    stash_guest = centred(splits[5], (SECTIONS, MICRO, EVICT, ROWS, BW), 1.0, 6.0, ((0, 2), (3, 16)))
    plan = draw_plan(jax.random.fold_in(splits[10], 71), 0)
    norm_gain = jnp.clip(1.0 + 0.15 * jax.random.normal(splits[7], (SECTIONS, D), jnp.float32), 0.25, 1.75)
    w_up = centred(splits[8], (SECTIONS, D, FF), D ** -0.5, 0.09375, ((0, 2), (1, 4), (2, 4)))
    w_down = centred(splits[9], (SECTIONS, FF, D), FF ** -0.5, 0.0546875, ((0, 2), (1, 4), (2, 4)))
    return dict(act_in=act_in, act_first=act_first, grad_in=grad_in, grad_last=grad_last, stash_local=stash_local, stash_guest=stash_guest, plan=plan, norm_gain=norm_gain, w_up=w_up, w_down=w_down)


EPSILON = 1e-05

def normalize(values, norm_scale):
    wide = values.astype(jnp.float32)
    inverse_rms = lax.rsqrt(lax.optimization_barrier(jnp.mean(wide * wide, axis=-1, keepdims=True)) + EPSILON)
    return (wide, inverse_rms, wide * inverse_rms * norm_scale)

def finish_norm(wide, inverse_rms, norm_scale, d_normed, cotangent):
    scaled = d_normed * norm_scale
    d_input = cotangent.astype(jnp.float32) + inverse_rms * scaled - wide * (inverse_rms * inverse_rms * inverse_rms) * lax.optimization_barrier(jnp.mean(scaled * wide, axis=-1, keepdims=True))
    return (d_input.astype(jnp.bfloat16), lax.optimization_barrier(jnp.sum(d_normed * wide * inverse_rms, axis=0)))

def local_grads(normed_low, cotangent, up_matrix, down_matrix):
    hidden_pre = jnp.dot(normed_low, up_matrix, preferred_element_type=jnp.float32)
    sigmoid_gate = jax.nn.sigmoid(hidden_pre)
    hidden = jax.nn.silu(hidden_pre).astype(jnp.bfloat16)
    d_hidden = lax.dot_general(cotangent, down_matrix, (((1,), (1,)), ((), ())), preferred_element_type=jnp.float32)
    d_pre = (d_hidden * sigmoid_gate * (1.0 + hidden_pre * (1.0 - sigmoid_gate))).astype(jnp.bfloat16)
    grad_down_part = lax.dot_general(hidden, cotangent, (((0,), (0,)), ((), ())), preferred_element_type=jnp.float32)
    grad_up_part = lax.dot_general(normed_low, d_pre, (((0,), (0,)), ((), ())), preferred_element_type=jnp.float32)
    return (d_pre, grad_up_part, grad_down_part)

def match_blocks(block_ids, block_count):
    return block_ids[:, None] == jnp.arange(block_count, dtype=jnp.int32)[None, :]

def pull_blocks(values, block_ids, block_width):
    row_total = values.shape[0]
    blocks = values.reshape(row_total, values.shape[1] // block_width, block_width)
    return jnp.transpose(jnp.take(blocks, block_ids, axis=1), (1, 0, 2))

def clear_blocks(values, block_ids, block_width):
    row_total = values.shape[0]
    block_count = values.shape[1] // block_width
    covered = jnp.any(match_blocks(block_ids, block_count), axis=0)
    blocks = values.reshape(row_total, block_count, block_width)
    return jnp.where(covered[None, :, None], jnp.zeros((), values.dtype), blocks).reshape(values.shape)

def place_blocks(values, block_ids, fetched):
    row_total = values.shape[0]
    block_width = fetched.shape[2]
    block_count = values.shape[1] // block_width
    matched = match_blocks(block_ids, block_count)
    covered = jnp.any(matched, axis=0)
    fetched_cols = jnp.einsum('eb,erw->rbw', matched.astype(jnp.float32), fetched.astype(jnp.float32))
    blocks = values.reshape(row_total, block_count, block_width).astype(jnp.float32)
    return jnp.where(covered[None, :, None], fetched_cols, blocks).reshape(values.shape).astype(values.dtype)

def forward(values, norm_scale, up_matrix, down_matrix):
    wide, inverse_rms, normed = normalize(values, norm_scale)
    hidden = jax.nn.silu(jnp.dot(normed.astype(jnp.bfloat16), up_matrix, preferred_element_type=jnp.float32)).astype(jnp.bfloat16)
    return (wide + jnp.dot(hidden, down_matrix, preferred_element_type=jnp.float32)).astype(jnp.bfloat16)

def backward(values, cotangent, norm_scale, up_matrix, down_matrix):
    wide, inverse_rms, normed = normalize(values, norm_scale)
    d_pre, grad_up_part, grad_down_part = local_grads(normed.astype(jnp.bfloat16), cotangent, up_matrix, down_matrix)
    d_normed = lax.dot_general(d_pre, up_matrix, (((1,), (1,)), ((), ())), preferred_element_type=jnp.float32)
    d_input, gain_part = finish_norm(wide, inverse_rms, norm_scale, d_normed, cotangent)
    return (d_input, gain_part, grad_up_part, grad_down_part)

def reference(act_in, act_first, grad_in, grad_last, stash_local, stash_guest, plan, norm_gain, w_up, w_down):
    layer_in = {}
    front = {}
    for position in range(SECTIONS):
        layer_in[position, 0] = act_in[position]
        front[position, 0] = forward(act_in[position], norm_gain[position], w_up[position], w_down[position])
    for position in range(SECTIONS):
        source = act_first if position == 0 else front[position - 1, 0]
        layer_in[position, 1] = source
        front[position, 1] = forward(source, norm_gain[position], w_up[position], w_down[position])

    def stashed(position, tick):
        own = stash_local[position, tick]
        if position >= HALF:
            return own
        holder = HALF + plan[0, tick, position, 0]
        return place_blocks(own, plan[0, tick, position, 1:], stash_guest[holder, tick])
    back = {}
    for position in range(SECTIONS):
        back[position, 0] = backward(stashed(position, 0), grad_in[position], norm_gain[position], w_up[position], w_down[position])
    for position in range(SECTIONS):
        cotangent = grad_last if position == SECTIONS - 1 else back[position + 1, 0][0]
        back[position, 1] = backward(stashed(position, 1), cotangent, norm_gain[position], w_up[position], w_down[position])
    act_out = jnp.stack([jnp.stack([front[position, 0], front[position, 1]]) for position in range(SECTIONS)])
    grad_out = jnp.stack([jnp.stack([back[position, 0][0], back[position, 1][0]]) for position in range(SECTIONS)])
    grad_gain = jnp.stack([back[position, 0][1] + back[position, 1][1] for position in range(SECTIONS)])
    grad_up = jnp.stack([(back[position, 0][2] + back[position, 1][2]).astype(jnp.bfloat16) for position in range(SECTIONS)])
    grad_down = jnp.stack([(back[position, 0][3] + back[position, 1][3]).astype(jnp.bfloat16) for position in range(SECTIONS)])
    keep_rows = []
    guest_rows = []
    for position in range(SECTIONS):
        keep_ticks = []
        guest_ticks = []
        for tick in range(MICRO):
            if position < HALF:
                keep_ticks.append(clear_blocks(layer_in[position, tick], plan[1, tick, position, 1:], BW))
                guest_ticks.append(jnp.zeros((EVICT, ROWS, BW), jnp.bfloat16))
            else:
                keep_ticks.append(layer_in[position, tick])
                gathered = jnp.zeros((EVICT, ROWS, BW), jnp.float32)
                for owner in range(HALF):
                    matched = plan[1, tick, owner, 0] + HALF == position
                    blocks = pull_blocks(layer_in[owner, tick], plan[1, tick, owner, 1:], BW).astype(jnp.float32)
                    gathered = gathered + jnp.where(matched, blocks, jnp.zeros((), jnp.float32))
                guest_ticks.append(gathered.astype(jnp.bfloat16))
        keep_rows.append(jnp.stack(keep_ticks))
        guest_rows.append(jnp.stack(guest_ticks))
    keep_out = jnp.stack(keep_rows)
    guest_out = jnp.stack(guest_rows)
    return (act_out, grad_out, keep_out, guest_out, grad_up, grad_down, grad_gain)
```

```python
import jax
import jax.numpy as jnp
from jax import lax
from jax.sharding import PartitionSpec as P

MICRO = 2


EPSILON = 1e-05


def passed_along(value, axis, steps):
    count = lax.axis_size(axis)
    first, last = (max(0, -steps), min(count, count - steps))
    return lax.ppermute(value, axis, [(source, source + steps) for source in range(first, last)])


def normalize(values, norm_scale):
    wide = values.astype(jnp.float32)
    inverse_rms = lax.rsqrt(jnp.mean(wide * wide, axis=-1, keepdims=True) + EPSILON)
    return (wide, inverse_rms, wide * inverse_rms * norm_scale)


def finish_norm(wide, inverse_rms, norm_scale, d_normed, cotangent):
    scaled = d_normed * norm_scale
    d_input = (
        cotangent.astype(jnp.float32)
        + inverse_rms * scaled
        - wide
        * (inverse_rms * inverse_rms * inverse_rms)
        * jnp.mean(scaled * wide, axis=-1, keepdims=True)
    )
    return (d_input.astype(jnp.bfloat16), jnp.sum(d_normed * wide * inverse_rms, axis=0))


def match_blocks(block_ids, block_count):
    return block_ids[:, None] == jnp.arange(block_count, dtype=jnp.int32)[None, :]


def pull_blocks(values, block_ids, block_width):
    row_total = values.shape[0]
    blocks = values.reshape(row_total, values.shape[1] // block_width, block_width)
    return jnp.transpose(jnp.take(blocks, block_ids, axis=1), (1, 0, 2))


def clear_blocks(values, block_ids, block_width):
    row_total = values.shape[0]
    block_count = values.shape[1] // block_width
    covered = jnp.any(match_blocks(block_ids, block_count), axis=0)
    blocks = values.reshape(row_total, block_count, block_width)
    return jnp.where(covered[None, :, None], jnp.zeros((), values.dtype), blocks).reshape(
        values.shape
    )


def place_blocks(values, block_ids, fetched):
    row_total = values.shape[0]
    block_width = fetched.shape[2]
    block_count = values.shape[1] // block_width
    matched = match_blocks(block_ids, block_count)
    covered = jnp.any(matched, axis=0)
    fetched_cols = jnp.einsum(
        "eb,erw->rbw", matched.astype(jnp.float32), fetched.astype(jnp.float32)
    )
    blocks = values.reshape(row_total, block_count, block_width).astype(jnp.float32)
    return (
        jnp.where(covered[None, :, None], fetched_cols, blocks)
        .reshape(values.shape)
        .astype(values.dtype)
    )


def settle(partial_value, row_count):
    tensor_count = lax.axis_size("tensor")
    shaped = partial_value.astype(jnp.bfloat16).reshape(
        tensor_count, -1, partial_value.shape[1]
    )
    arrived = lax.all_to_all(shaped, "tensor", split_axis=0, concat_axis=0, tiled=True)
    reduced = jnp.sum(arrived.astype(jnp.float32), axis=0).astype(jnp.bfloat16)
    placed = lax.all_to_all(reduced, "dp", split_axis=0, concat_axis=1, tiled=True)
    return placed.reshape(row_count, -1).astype(jnp.float32)


def after(value, earlier):
    return lax.optimization_barrier((value, earlier))[0]


def spread(values):
    exchanged = lax.all_to_all(values, "dp", split_axis=1, concat_axis=0, tiled=True)
    return lax.all_gather(exchanged, "tensor", axis=0, tiled=True)


def sum_over_blocks(partial_value):
    return lax.psum_scatter(
        partial_value.astype(jnp.bfloat16), "dp", scatter_dimension=0, tiled=True
    ).astype(jnp.float32)


def project_up(row_block, up_matrix):
    return sum_over_blocks(jnp.dot(row_block, up_matrix, preferred_element_type=jnp.float32))


def forward_finish(wide, hidden, down_matrix):
    partial_value = jnp.dot(
        lax.all_gather(hidden, "dp", axis=0, tiled=True),
        down_matrix,
        preferred_element_type=jnp.float32,
    )
    return (wide + settle(partial_value, wide.shape[0])).astype(jnp.bfloat16)


def normed_rows(values, norm_scale):
    wide, inverse_rms, normed = normalize(values, norm_scale)
    return (wide, inverse_rms, spread(normed.astype(jnp.bfloat16)))


def hidden_rows(hidden_pre):
    return jax.nn.silu(hidden_pre).astype(jnp.bfloat16)


def hidden_back(cotan_block, down_matrix):
    return sum_over_blocks(
        lax.dot_general(
            cotan_block, down_matrix, (((1,), (1,)), ((), ())), preferred_element_type=jnp.float32
        )
    )


def pre_grad(hidden_pre, d_hidden):
    sigmoid_gate = jax.nn.sigmoid(hidden_pre)
    return (d_hidden * sigmoid_gate * (1.0 + hidden_pre * (1.0 - sigmoid_gate))).astype(
        jnp.bfloat16
    )


def backward_finish(d_pre_piece, wide, inverse_rms, cotangent, norm_scale, up_matrix):
    normed_part = lax.dot_general(
        d_pre_piece, up_matrix, (((1,), (1,)), ((), ())), preferred_element_type=jnp.float32
    )
    d_normed = settle(normed_part, cotangent.shape[0])
    return finish_norm(wide, inverse_rms, norm_scale, d_normed, cotangent)


def weight_grad(first, second):
    left = jnp.concatenate([first[0], second[0]], axis=0)
    right = jnp.concatenate([first[1], second[1]], axis=0)
    return lax.dot_general(
        left, right, (((0,), (0,)), ((), ())), preferred_element_type=jnp.float32
    ).astype(jnp.bfloat16)


def local(
    act_in, act_first, grad_in, grad_last, stash_local, stash_guest, plan, norm_gain, w_up, w_down
):
    section_count = lax.axis_size("pipe")
    half_sections = section_count // 2
    section_index = lax.axis_index("pipe")
    is_early = section_index < half_sections
    plan_row = jnp.minimum(section_index, half_sections - 1)
    block_width = stash_guest.shape[-1]
    norm_scale = norm_gain[0]
    up_matrix = w_up[0]
    down_matrix = w_down[0]
    section_ids = jnp.arange(section_count, dtype=jnp.int32)
    clipped_ids = jnp.minimum(section_ids, half_sections - 1)
    section_early = section_ids < half_sections
    zero_low = jnp.zeros((), jnp.bfloat16)
    old_holder = plan[0, :, :, 0] + half_sections
    sends_back = section_early[:, None] & (
        jnp.transpose(old_holder[:, clipped_ids]) == section_index
    )
    outgoing = jnp.where(sends_back[:, :, None, None, None], stash_guest[0][None], zero_low)
    source_pick = section_ids[:, None] == old_holder[:, plan_row][None, :]
    fetched_list = []
    for tick in range(MICRO):
        arrived = lax.all_to_all(outgoing[:, tick], "pipe", split_axis=0, concat_axis=0, tiled=True)
        fetched_list.append(
            jnp.sum(jnp.where(source_pick[:, tick, None, None, None], arrived, zero_low), axis=0)
        )
    stash_rows = []
    for tick in range(MICRO):
        own = stash_local[0, tick]
        merged = place_blocks(own, plan[0, tick, plan_row, 1:], fetched_list[tick])
        stash_rows.append(jnp.where(is_early, merged, own))
    wide_b0, rms_b0, block_b0 = normed_rows(stash_rows[0], norm_scale)
    cot_block_b0 = spread(grad_in[0])
    pre_b0 = project_up(block_b0, up_matrix)
    d_pre_b0 = pre_grad(pre_b0, hidden_back(cot_block_b0, down_matrix))
    wide_f0, _, block_f0 = normed_rows(act_in[0], norm_scale)
    pre_f0 = project_up(after(block_f0, d_pre_b0), up_matrix)
    piece_b0 = lax.all_gather(d_pre_b0, "dp", axis=0, tiled=True)
    back_zero = backward_finish(piece_b0, wide_b0, rms_b0, grad_in[0], norm_scale, up_matrix)
    returned = passed_along(back_zero[0], "pipe", -1)
    cot_one = jnp.where(section_index == section_count - 1, grad_last, returned)
    cot_block_b1 = spread(cot_one)
    front_zero = forward_finish(wide_f0, after(hidden_rows(pre_f0), cot_block_b1), down_matrix)
    wide_b1, rms_b1, block_b1 = normed_rows(stash_rows[1], norm_scale)
    pre_b1 = project_up(after(block_b1, cot_block_b1), up_matrix)
    d_pre_b1 = pre_grad(pre_b1, hidden_back(cot_block_b1, down_matrix))
    passed = passed_along(front_zero, "pipe", 1)
    input_one = jnp.where(section_index == 0, act_first, passed)
    wide_f1, _, block_f1 = normed_rows(input_one, norm_scale)
    pre_f1 = project_up(block_f1, up_matrix)
    piece_b1 = lax.all_gather(d_pre_b1, "dp", axis=0, tiled=True)
    back_one = backward_finish(piece_b1, wide_b1, rms_b1, cot_one, norm_scale, up_matrix)
    front_one = forward_finish(wide_f1, after(hidden_rows(pre_f1), piece_b1), down_matrix)
    hidden_b0, hidden_b1 = (
        lax.all_gather(after(hidden_rows(pre), piece_b1), "dp", axis=0, tiled=True)
        for pre in (pre_b0, pre_b1)
    )
    gain_grad = jnp.sum(
        lax.all_gather(back_zero[1] + back_one[1], ("dp", "tensor"), axis=0), axis=0
    )
    new_inputs = [act_in[0], input_one]
    new_holder = plan[1, :, :, 0] + half_sections
    pulled = jnp.stack(
        [
            pull_blocks(new_inputs[tick], plan[1, tick, plan_row, 1:], block_width)
            for tick in range(MICRO)
        ]
    )
    heading = is_early & (section_ids[:, None] == new_holder[:, plan_row][None, :])
    parcels = jnp.where(heading[:, :, None, None, None], pulled[None], zero_low)
    landed = lax.all_to_all(parcels, "pipe", split_axis=0, concat_axis=0, tiled=True)
    coming = section_early[:, None] & (jnp.transpose(new_holder[:, clipped_ids]) == section_index)
    guest_new = jnp.sum(jnp.where(coming[:, :, None, None, None], landed, zero_low), axis=0)
    kept = jnp.stack(
        [
            jnp.where(
                is_early,
                clear_blocks(new_inputs[tick], plan[1, tick, plan_row, 1:], block_width),
                new_inputs[tick],
            )
            for tick in range(MICRO)
        ]
    )
    act_out = jnp.stack([front_zero, front_one])[None]
    grad_out = jnp.stack([back_zero[0], back_one[0]])[None]
    grad_up = weight_grad((block_b0, piece_b0), (block_b1, piece_b1))[None]
    grad_down = weight_grad((hidden_b0, cot_block_b0), (hidden_b1, cot_block_b1))[None]
    return (act_out, grad_out, kept[None], guest_new[None], grad_up, grad_down, gain_grad[None])


def solution(mesh):
    placed = (
        P("pipe", ("dp", "tensor"), None),
        P(("dp", "tensor"), None),
        P("pipe", ("dp", "tensor"), None),
        P(("dp", "tensor"), None),
        P("pipe", None, ("dp", "tensor"), None),
        P("pipe", None, None, ("dp", "tensor"), None),
        P(),
        P("pipe", None),
        P("pipe", "dp", "tensor"),
        P("pipe", "tensor", "dp"),
    )
    return jax.shard_map(
        local,
        mesh=mesh,
        in_specs=placed,
        out_specs=(
            P("pipe", None, ("dp", "tensor"), None),
            P("pipe", None, ("dp", "tensor"), None),
            P("pipe", None, ("dp", "tensor"), None),
            P("pipe", None, None, ("dp", "tensor"), None),
            P("pipe", "dp", "tensor"),
            P("pipe", "tensor", "dp"),
            P("pipe", None),
        ),
        check_vma=False,
    )
```
